512 devices in a mesh: row: 16 (over x_hi, y, core), col: 32 (over z, x_lo).
Axes of the slice: x: 4 (x_hi: 2, x_lo: 2; x = x_hi * 2 + x_lo), y: 4, z: 16, core: 2. Of those that a mesh axis runs over, the one named last changes fastest.
Arguments:
- orbitals: bfloat16 [16384, 2048], P(('row', 'col')), may hold values from -0.125 to 0.125
- coulomb: bfloat16 [16384, 16384], P('row', 'col'), may hold values from -6 to 6
- applied: bfloat16 [16384, 256], P(('row', 'col')), may hold values from -6 to 6
Outputs:
- projectors: float32 [16384, 256], P(('row', 'col'))
The draws below stay inside these ranges and needn't reach their ends.
All inputs are finite; a program needn't handle non-finite values.
Results may differ from the reference program's by a relative error of at most 0.0029.
Values may be sent and summed in bfloat16 or wider, within the bound.
No kernel may reach another device: no remote copies, remote signals or barrier semaphores. Data moves between devices by JAX's collectives and lax.ppermute only.
A program may use at most 64 MiB of HBM per device.

```python
import jax
import jax.numpy as jnp
from jax import lax

NMU = 16384
NAPP = 256
NOCC = 2048
N_ROW = 16
N_COL = 32


def spiked(values, key, source, target, parts, factor):
    owner, partner = [(jnp.arange(values.shape[dim]) // (values.shape[dim] // parts)).reshape([-1 if axis == dim else 1 for axis in range(values.ndim)]) for dim in (source, target)]
    chosen = jax.random.permutation(key, parts)[partner]
    strong = (owner == chosen) | (owner == (partner + parts // 2) % parts)
    return jnp.where(strong, factor * values, values)


def block_levels(stream_key, shape, cuts, smallest, largest):
    gain, own = 1.0, jax.random.fold_in(stream_key, 6)
    for dim, blocks in cuts:
        draws = jnp.exp(jax.random.uniform(jax.random.fold_in(own, dim), (blocks,), jnp.float32, smallest / len(cuts), largest / len(cuts)))
        gain = gain * jnp.repeat(draws, shape[dim] // blocks).reshape([-1 if axis == dim else 1 for axis in range(len(shape))])
    return gain


def noise(stream_key, dims, deviation, reach, split=(), kind=jnp.bfloat16):
    drawn = jax.random.normal(stream_key, dims, jnp.float32) * deviation
    if len(split) > 0:
        drawn = block_levels(stream_key, dims, split, -0.22, 0.18) * drawn
    return jnp.clip(drawn, min=-reach, max=reach).astype(kind)


def gaussian_with(rng, shape, spread, limit, split, heavy, kind=jnp.bfloat16):
    array = spread * jax.random.normal(rng, shape, jnp.float32)
    if split:
        array = array * block_levels(rng, shape, split, -0.22, 0.18)
    return jnp.clip(spiked(array, jax.random.fold_in(rng, 3), *heavy), -limit, limit).astype(kind)


def setup_inputs(seed: int = 0) -> dict:
    arg_keys = jax.random.split(jax.random.key(seed), 4)
    return {
        "orbitals": noise(arg_keys[0], (NMU, NOCC), NOCC ** -0.5, 0.125, ((0, 512),)),
        "coulomb": gaussian_with(arg_keys[1], (NMU, NMU), 1.0, 6.0, ((0, 16), (1, 32)), (1, 0, 32, 2.75)),
        "applied": noise(arg_keys[2], (NMU, NAPP), 1.0, 6.0, ((0, 512),)),
    }


def permute_points(matrix):
    point_count = NMU // (N_ROW * N_COL)
    shaped = matrix.reshape(N_ROW, N_COL, point_count, matrix.shape[1])
    return jnp.transpose(shaped, (1, 0, 2, 3)).reshape(NMU, matrix.shape[1])

def reference(orbitals, coulomb, applied):
    orbit_wide = orbitals.astype(jnp.float32)
    paired = permute_points(orbit_wide)
    paired_applied = permute_points(applied.astype(jnp.float32))
    block_rows = 1024 if NMU % 1024 == 0 else NMU

    def one_block(block_index):
        row_slab = lax.dynamic_slice_in_dim(orbit_wide, block_index * block_rows, block_rows, 0)
        coulomb_slab = lax.dynamic_slice_in_dim(coulomb, block_index * block_rows, block_rows, 0).astype(jnp.float32)
        density = jnp.dot(row_slab, paired.T, precision=lax.Precision.HIGHEST)
        kernel = (coulomb_slab * density).astype(jnp.bfloat16)
        kernel = lax.optimization_barrier(kernel).astype(jnp.float32)
        return jnp.dot(kernel, paired_applied, precision=lax.Precision.HIGHEST)
    images = lax.map(one_block, jnp.arange(NMU // block_rows, dtype=jnp.int32))
    images = images.reshape(NMU, NAPP)
    gram_sum = jnp.dot(images.T, images, precision=lax.Precision.HIGHEST)
    gram_matrix = jnp.eye(NAPP, dtype=jnp.float32) + gram_sum / NMU
    factor = jnp.linalg.cholesky(gram_matrix)
    projectors = lax.linalg.triangular_solve(factor, images, left_side=False, lower=True, transpose_a=True)
    return projectors
```

```python
import jax
import jax.numpy as jnp
from jax import lax
from jax.sharding import PartitionSpec as P

NMU = 16384
BOTH = ("row", "col")


def reduce_rows(partial):
    n = lax.axis_size("col")
    chunks = partial.astype(jnp.bfloat16).reshape(n, -1, partial.shape[1])
    moved = lax.all_to_all(chunks, "col", 0, 0, tiled=True)
    return jnp.sum(moved.astype(jnp.float32), axis=0)


def sum_everywhere(x):
    n = lax.axis_size("row") * lax.axis_size("col")
    chunks = x.reshape(n, 1, -1)
    share = jnp.sum(lax.all_to_all(chunks, BOTH, 0, 0, tiled=True), axis=0)
    copies = jnp.broadcast_to(share[None], chunks.shape)
    return lax.all_to_all(copies, BOTH, 0, 0, tiled=True).reshape(x.shape)


def per_device(orbitals, coulomb, applied):
    point_block = lax.all_gather(orbitals, "col", axis=0, tiled=True)
    paired_orbitals, paired_applied = (
        lax.all_gather(orbitals, "row", axis=0, tiled=True),
        lax.all_gather(applied, "row", axis=0, tiled=True),
    )
    density = jnp.einsum(
        "ik,jk->ij", point_block, paired_orbitals, preferred_element_type=jnp.float32
    )
    kernel = (coulomb.astype(jnp.float32) * density).astype(jnp.bfloat16)
    images = reduce_rows(
        jnp.dot(kernel, paired_applied, preferred_element_type=jnp.float32)
    )
    local_gram = jnp.einsum("ia,ib->ab", images, images, precision=lax.Precision.HIGHEST)
    gram_sum = sum_everywhere(local_gram)
    gram_matrix = jnp.eye(gram_sum.shape[0], dtype=jnp.float32) + gram_sum / NMU
    factor = jnp.linalg.cholesky(gram_matrix)
    projectors = lax.linalg.triangular_solve(
        factor, images, left_side=False, lower=True, transpose_a=True
    )
    return projectors


def solution(mesh):
    return jax.shard_map(
        per_device,
        mesh=mesh,
        in_specs=(P(("row", "col"), None), P("row", "col"), P(("row", "col"), None)),
        out_specs=P(("row", "col"), None),
        check_vma=False,
    )
```

```python
import jax
import jax.numpy as jnp
from jax import lax
from jax.sharding import Mesh
from jax.sharding import PartitionSpec as P

NMU = 16384
ROW = ("x_hi", "y", "core")
COL = ("z", "x_lo")
PLANE = ("x_hi", "y", "core", "x_lo")
AXES = ROW + COL
SIZES = (2, 4, 2, 16, 2)


def exchange(chunks, axes):
    return lax.all_to_all(chunks, axes, 0, 0, tiled=True)


def spread(x, axes):
    copies = jnp.broadcast_to(x[None], (lax.axis_size(axes),) + x.shape)
    return exchange(copies, axes)


def gather_col(orbitals):
    n = lax.axis_size("z")
    z = lax.axis_index("z")
    pair = spread(orbitals, "x_lo").reshape(-1, orbitals.shape[1])
    rows = pair.shape[0]
    block = jnp.zeros((n * rows, pair.shape[1]), pair.dtype)
    block = lax.dynamic_update_slice(block, pair, (z * rows, 0))
    up = [(i, (i + 1) % n) for i in range(n)]
    down = [(i, (i - 1) % n) for i in range(n)]
    ahead, behind = pair, pair
    for step in range(1, n // 2 + 1):
        ahead = lax.ppermute(ahead, "z", up)
        if step < n // 2:
            behind = lax.ppermute(behind, "z", down)
            block = lax.dynamic_update_slice(block, behind, (((z + step) & (n - 1)) * rows, 0))
        block = lax.dynamic_update_slice(block, ahead, (((z - step) & (n - 1)) * rows, 0))
    return block


def reduce_rows(partial):
    chunks = partial.astype(jnp.bfloat16).reshape(lax.axis_size(COL), -1, partial.shape[1])
    return jnp.sum(exchange(chunks, COL).astype(jnp.float32), axis=0)


def sum_everywhere(x):
    n = lax.axis_size(PLANE)
    share = jnp.sum(exchange(x.reshape(n, -1, x.shape[1]), PLANE), axis=0)
    share = jnp.sum(spread(share, "z"), axis=0)
    return spread(share, PLANE).reshape(x.shape)


def per_device(orbitals, coulomb, applied):
    width = orbitals.shape[1]
    paired = spread(jnp.concatenate([orbitals, applied], axis=1), ROW)
    paired = paired.reshape(-1, paired.shape[-1])
    paired_orbitals, paired_applied = paired[:, :width], paired[:, width:]
    point_block = gather_col(orbitals)
    density = jnp.einsum(
        "ik,jk->ij", point_block, paired_orbitals, preferred_element_type=jnp.float32
    )
    kernel = (coulomb.astype(jnp.float32) * density).astype(jnp.bfloat16)
    images = reduce_rows(
        jnp.dot(kernel, paired_applied, preferred_element_type=jnp.float32)
    )
    local_gram = jnp.einsum("ia,ib->ab", images, images, precision=lax.Precision.HIGHEST)
    gram_sum = sum_everywhere(local_gram)
    gram_matrix = jnp.eye(gram_sum.shape[0], dtype=jnp.float32) + gram_sum / NMU
    factor = jnp.linalg.cholesky(gram_matrix)
    projectors = lax.linalg.triangular_solve(
        factor, images, left_side=False, lower=True, transpose_a=True
    )
    return projectors


def solution(mesh):
    fine = Mesh(mesh.devices.reshape(SIZES), AXES)
    return jax.shard_map(
        per_device,
        mesh=fine,
        in_specs=(P(AXES, None), P(ROW, COL), P(AXES, None)),
        out_specs=P(AXES, None),
        check_vma=False,
    )
```

```python
import functools

import jax
import jax.numpy as jnp
from jax import lax
from jax.experimental import pallas as pl
from jax.experimental.pallas import tpu as pltpu
from jax.sharding import Mesh
from jax.sharding import PartitionSpec as P

NMU = 16384
ROW = ("x_hi", "y", "core")
COL = ("z", "x_lo")
PLANE = ("x_hi", "y", "core", "x_lo")
AXES = ROW + COL
SIZES = (2, 4, 2, 16, 2)


def exchange(chunks, axes):
    return lax.all_to_all(chunks, axes, 0, 0, tiled=True)


def spread(x, axes):
    copies = jnp.broadcast_to(x[None], (lax.axis_size(axes),) + x.shape)
    return exchange(copies, axes)


def gather_col(orbitals):
    n = lax.axis_size("z")
    z = lax.axis_index("z")
    pair = spread(orbitals, "x_lo").reshape(-1, orbitals.shape[1])
    rows = pair.shape[0]
    block = jnp.zeros((n * rows, pair.shape[1]), pair.dtype)
    block = lax.dynamic_update_slice(block, pair, (z * rows, 0))
    up = [(i, (i + 1) % n) for i in range(n)]
    down = [(i, (i - 1) % n) for i in range(n)]
    ahead, behind = pair, pair
    for step in range(1, n // 2 + 1):
        ahead = lax.ppermute(ahead, "z", up)
        if step < n // 2:
            behind = lax.ppermute(behind, "z", down)
            block = lax.dynamic_update_slice(block, behind, (((z + step) & (n - 1)) * rows, 0))
        block = lax.dynamic_update_slice(block, ahead, (((z - step) & (n - 1)) * rows, 0))
    return block


def reduce_rows(partial):
    chunks = partial.astype(jnp.bfloat16).reshape(lax.axis_size(COL), -1, partial.shape[1])
    return jnp.sum(exchange(chunks, COL).astype(jnp.float32), axis=0)


def sum_everywhere(x):
    n = lax.axis_size(PLANE)
    share = jnp.sum(exchange(x.reshape(n, -1, x.shape[1]), PLANE), axis=0)
    share = jnp.sum(spread(share, "z"), axis=0)
    return spread(share, PLANE).reshape(x.shape)


def wide(value, width):
    return jnp.concatenate([value] * (width // 128), axis=1)


def eliminate(groups, lane, step):
    width = groups[0].shape[1]
    sublane = lax.broadcasted_iota(jnp.int32, (8, 1), 0)
    for j in range(0, 8 * len(groups), step):
        home, first = j // 8, j % 8
        own = groups[home]
        low = [[None] * step for _ in range(step)]
        scales = []
        for b in range(step):
            at = lane + j + b
            column = jnp.broadcast_to(own[:, at : at + 1], (8, 128))
            for a in range(b, step):
                v = jnp.broadcast_to(column[first + a : first + a + 1, :], (8, 128))
                for c in range(b):
                    v = v - low[a][c] * low[b][c]
                if a == b:
                    scales.append(lax.rsqrt(v))
                else:
                    low[a][b] = v * scales[b]
        rows = []
        for a in range(step):
            v = jnp.broadcast_to(own[first + a : first + a + 1, :], (8, width))
            for c in range(a):
                v = v - wide(low[a][c], width) * rows[c]
            rows.append(v * wide(scales[a], width))
        for g in range(home, len(groups)):
            value = groups[g]
            if g > home or first + step < 8:
                columns = []
                new = value
                for b in range(step):
                    at = lane + j + b
                    v = jnp.broadcast_to(value[:, at : at + 1], (8, 128))
                    for c in range(b):
                        v = v - columns[c] * low[b][c]
                    columns.append(v * scales[b])
                    new = new - wide(columns[b], width) * rows[b]
                value = jnp.where(sublane >= first + step, new, value) if g == home else new
            if g == home:
                for a in range(step):
                    value = jnp.where(sublane == first + a, rows[a], value)
            groups[g] = value
    return groups


def orthonormalize_kernel(block, step, gram_ref, images_ref, out_ref, work, upper):
    n, m = gram_ref.shape[0], images_ref.shape[0]
    rows = lax.broadcasted_iota(jnp.int32, (n, n), 0)
    cols = lax.broadcasted_iota(jnp.int32, (n, n), 1)
    work[:, :n] = gram_ref[...] * (1 / NMU) + jnp.where(rows == cols, 1.0, 0.0)
    padding = jnp.zeros((128 - m, n), jnp.float32)
    work[:, n:] = jnp.concatenate([images_ref[...], padding], axis=0).T
    for k in range(0, n, block):
        t = k // 128 * 128
        groups = [work[k + g : k + g + 8, t:] for g in range(0, block, 8)]
        done = jnp.concatenate(eliminate(groups, k - t, step), axis=0)
        upper[k : k + block, :] = done[:, n - t :]
        r = (k + block) // 128 * 128
        if k + block < n:
            work[r:, r:] -= lax.dot_general(
                done[:, r - t : n - t],
                done[:, r - t :],
                (((0,), (0,)), ((), ())),
                precision=lax.Precision.HIGHEST,
                preferred_element_type=jnp.float32,
            )
    out_ref[...] = upper[...].T[:m, :]


def orthonormalize(gram_sum, images):
    n, m = gram_sum.shape[0], images.shape[0]
    return pl.pallas_call(
        functools.partial(orthonormalize_kernel, 64, 8),
        out_shape=jax.ShapeDtypeStruct((m, n), jnp.float32),
        in_specs=[pl.BlockSpec(memory_space=pltpu.VMEM)] * 2,
        out_specs=pl.BlockSpec(memory_space=pltpu.VMEM),
        scratch_shapes=[
            pltpu.VMEM((n, n + 128), jnp.float32),
            pltpu.VMEM((n, 128), jnp.float32),
        ],
    )(gram_sum, images)


def per_device(orbitals, coulomb, applied):
    width = orbitals.shape[1]
    paired = spread(jnp.concatenate([orbitals, applied], axis=1), ROW)
    paired = paired.reshape(-1, paired.shape[-1])
    paired_orbitals, paired_applied = paired[:, :width], paired[:, width:]
    point_block = gather_col(orbitals)
    density = jnp.einsum(
        "ik,jk->ij", point_block, paired_orbitals, preferred_element_type=jnp.float32
    )
    kernel = (coulomb.astype(jnp.float32) * density).astype(jnp.bfloat16)
    images = reduce_rows(
        jnp.dot(kernel, paired_applied, preferred_element_type=jnp.float32)
    )
    local_gram = jnp.einsum("ia,ib->ab", images, images, precision=lax.Precision.HIGHEST)
    return orthonormalize(sum_everywhere(local_gram), images)


def solution(mesh):
    fine = Mesh(mesh.devices.reshape(SIZES), AXES)
    return jax.shard_map(
        per_device,
        mesh=fine,
        in_specs=(P(AXES, None), P(ROW, COL), P(AXES, None)),
        out_specs=P(AXES, None),
        check_vma=False,
    )
```

```python
import functools

import jax
import jax.numpy as jnp
from jax import lax
from jax.experimental import pallas as pl
from jax.experimental.pallas import tpu as pltpu
from jax.sharding import Mesh
from jax.sharding import PartitionSpec as P

NMU = 16384
ROW = ("x_hi", "y", "core")
COL = ("z", "x_lo")
PLANE = ("x_lo",) + ROW
AXES = ROW + COL
SIZES = (2, 4, 2, 16, 2)


def exchange(chunks, axes):
    return lax.all_to_all(chunks, axes, 0, 0, tiled=True)


def spread(x, axes):
    copies = jnp.broadcast_to(x[None], (lax.axis_size(axes),) + x.shape)
    return exchange(copies, axes)


def gather_z(mine):
    n = lax.axis_size("z")
    z = lax.axis_index("z")
    rows = mine.shape[0]
    block = jnp.zeros((n * rows, mine.shape[1]), mine.dtype)
    block = lax.dynamic_update_slice(block, mine, (z * rows, 0))
    up = [(i, (i + 1) % n) for i in range(n)]
    down = [(i, (i - 1) % n) for i in range(n)]
    ahead, behind = mine, mine
    for step in range(1, n // 2 + 1):
        ahead = lax.ppermute(ahead, "z", up)
        if step < n // 2:
            behind = lax.ppermute(behind, "z", down)
            block = lax.dynamic_update_slice(block, behind, (((z + step) & (n - 1)) * rows, 0))
        block = lax.dynamic_update_slice(block, ahead, (((z - step) & (n - 1)) * rows, 0))
    return block


def swap_sides(coulomb, count):
    side = lax.axis_index("x_lo")
    halves = coulomb.reshape(-1, 2, count, coulomb.shape[1])
    first, second = halves[:, 0], halves[:, 1]
    low = side == 0
    kept = jnp.where(low, first, second)
    moved = lax.ppermute(jnp.where(low, second, first), "x_lo", [(0, 1), (1, 0)])
    left, right = jnp.where(low, kept, moved), jnp.where(low, moved, kept)
    return jnp.concatenate([left, right], axis=-1).reshape(-1, 2 * coulomb.shape[1])


def reduce_rows(partial):
    chunks = partial.astype(jnp.bfloat16).reshape(lax.axis_size("z"), -1, partial.shape[1])
    return jnp.sum(exchange(chunks, "z").astype(jnp.float32), axis=0)


def sum_everywhere(x):
    n = lax.axis_size(PLANE)
    share = jnp.sum(exchange(x.reshape(n, -1, x.shape[1]), PLANE), axis=0)
    share = jnp.sum(spread(share, "z"), axis=0)
    return spread(share, PLANE).reshape(x.shape)


def wide(value, width):
    return jnp.concatenate([value] * (width // 128), axis=1)


def eliminate(groups, lane, step):
    width = groups[0].shape[1]
    sublane = lax.broadcasted_iota(jnp.int32, (8, 1), 0)
    for j in range(0, 8 * len(groups), step):
        home, first = j // 8, j % 8
        own = groups[home]
        low = [[None] * step for _ in range(step)]
        scales = []
        for b in range(step):
            at = lane + j + b
            column = jnp.broadcast_to(own[:, at : at + 1], (8, 128))
            for a in range(b, step):
                v = jnp.broadcast_to(column[first + a : first + a + 1, :], (8, 128))
                for c in range(b):
                    v = v - low[a][c] * low[b][c]
                if a == b:
                    scales.append(lax.rsqrt(v))
                else:
                    low[a][b] = v * scales[b]
        rows = []
        for a in range(step):
            v = jnp.broadcast_to(own[first + a : first + a + 1, :], (8, width))
            for c in range(a):
                v = v - wide(low[a][c], width) * rows[c]
            rows.append(v * wide(scales[a], width))
        for g in range(home, len(groups)):
            value = groups[g]
            if g > home or first + step < 8:
                columns = []
                new = value
                for b in range(step):
                    at = lane + j + b
                    v = jnp.broadcast_to(value[:, at : at + 1], (8, 128))
                    for c in range(b):
                        v = v - columns[c] * low[b][c]
                    columns.append(v * scales[b])
                    new = new - wide(columns[b], width) * rows[b]
                value = jnp.where(sublane >= first + step, new, value) if g == home else new
            if g == home:
                for a in range(step):
                    value = jnp.where(sublane == first + a, rows[a], value)
            groups[g] = value
    return groups


def orthonormalize_kernel(block, step, gram_ref, images_ref, out_ref, work, upper):
    n, m = gram_ref.shape[0], images_ref.shape[0]
    rows = lax.broadcasted_iota(jnp.int32, (n, n), 0)
    cols = lax.broadcasted_iota(jnp.int32, (n, n), 1)
    work[:, :n] = gram_ref[...] * (1 / NMU) + jnp.where(rows == cols, 1.0, 0.0)
    padding = jnp.zeros((128 - m, n), jnp.float32)
    work[:, n:] = jnp.concatenate([images_ref[...], padding], axis=0).T
    for k in range(0, n, block):
        t = k // 128 * 128
        groups = [work[k + g : k + g + 8, t:] for g in range(0, block, 8)]
        done = jnp.concatenate(eliminate(groups, k - t, step), axis=0)
        upper[k : k + block, :] = done[:, n - t :]
        r = (k + block) // 128 * 128
        if k + block < n:
            work[r:, r:] -= lax.dot_general(
                done[:, r - t : n - t],
                done[:, r - t :],
                (((0,), (0,)), ((), ())),
                precision=lax.Precision.HIGHEST,
                preferred_element_type=jnp.float32,
            )
    out_ref[...] = upper[...].T[:m, :]


def orthonormalize(gram_sum, images):
    n, m = gram_sum.shape[0], images.shape[0]
    return pl.pallas_call(
        functools.partial(orthonormalize_kernel, 64, 8),
        out_shape=jax.ShapeDtypeStruct((m, n), jnp.float32),
        in_specs=[pl.BlockSpec(memory_space=pltpu.VMEM)] * 2,
        out_specs=pl.BlockSpec(memory_space=pltpu.VMEM),
        scratch_shapes=[
            pltpu.VMEM((n, n + 128), jnp.float32),
            pltpu.VMEM((n, 128), jnp.float32),
        ],
    )(gram_sum, images)


def per_device(orbitals, coulomb, applied):
    width = orbitals.shape[1]
    paired = spread(jnp.concatenate([orbitals, applied], axis=1), PLANE)
    paired = paired.reshape(-1, paired.shape[-1])
    tile = swap_sides(coulomb, orbitals.shape[0])
    points = gather_z(orbitals)
    density = jnp.einsum(
        "ik,jk->ij", points, paired[:, :width], preferred_element_type=jnp.float32
    )
    kernel = (tile.astype(jnp.float32) * density).astype(jnp.bfloat16)
    images = reduce_rows(
        jnp.dot(kernel, paired[:, width:], preferred_element_type=jnp.float32)
    )
    local_gram = jnp.einsum("ia,ib->ab", images, images, precision=lax.Precision.HIGHEST)
    return orthonormalize(sum_everywhere(local_gram), images)


def solution(mesh):
    fine = Mesh(mesh.devices.reshape(SIZES), AXES)
    return jax.shard_map(
        per_device,
        mesh=fine,
        in_specs=(P(AXES, None), P(ROW, COL), P(AXES, None)),
        out_specs=P(AXES, None),
        check_vma=False,
    )
```

```python
import functools

import jax
import jax.numpy as jnp
from jax import lax
from jax.experimental import pallas as pl
from jax.experimental.pallas import tpu as pltpu
from jax.sharding import Mesh
from jax.sharding import PartitionSpec as P

NMU = 16384
ROW = ("x_hi", "y", "core")
COL = ("z", "x_lo")
PLANE = ("x_lo",) + ROW
AXES = ROW + COL
SIZES = (2, 4, 2, 16, 2)


def exchange(chunks, axes):
    return lax.all_to_all(chunks, axes, 0, 0, tiled=True)


def spread(x, axes):
    copies = jnp.broadcast_to(x[None], (lax.axis_size(axes),) + x.shape)
    return exchange(copies, axes)


def after(value, *others):
    return lax.optimization_barrier((value,) + others)[0]


def gather_z(mine):
    n = lax.axis_size("z")
    z = lax.axis_index("z")
    rows = mine.shape[0]
    block = jnp.zeros((n * rows, mine.shape[1]), mine.dtype)
    block = lax.dynamic_update_slice(block, mine, (z * rows, 0))
    up = [(i, (i + 1) % n) for i in range(n)]
    down = [(i, (i - 1) % n) for i in range(n)]
    ahead, behind = mine, mine
    for step in range(1, n // 2 + 1):
        ahead = lax.ppermute(ahead, "z", up)
        if step < n // 2:
            behind = lax.ppermute(behind, "z", down)
            block = lax.dynamic_update_slice(block, behind, (((z + step) & (n - 1)) * rows, 0))
            late = behind
        block = lax.dynamic_update_slice(block, ahead, (((z - step) & (n - 1)) * rows, 0))
    return block, late


def swap_sides(coulomb, count, late):
    side = lax.axis_index("x_lo")
    halves = coulomb.reshape(-1, 2, count, coulomb.shape[1])
    first, second = halves[:, 0], halves[:, 1]
    low = side == 0
    kept = jnp.where(low, first, second)
    moved = lax.ppermute(jnp.where(low, second, first), "x_lo", [(0, 1), (1, 0)])
    moved = after(moved, late)
    left, right = jnp.where(low, kept, moved), jnp.where(low, moved, kept)
    return jnp.concatenate([left, right], axis=-1).reshape(-1, 2 * coulomb.shape[1])


def reduce_rows(partial):
    chunks = partial.astype(jnp.bfloat16).reshape(lax.axis_size("z"), -1, partial.shape[1])
    return jnp.sum(exchange(chunks, "z").astype(jnp.float32), axis=0)


def sum_everywhere(x):
    n = lax.axis_size(PLANE)
    share = jnp.sum(exchange(x.reshape(n, -1, x.shape[1]), PLANE), axis=0)
    share = jnp.sum(spread(share, "z"), axis=0)
    return spread(share, PLANE).reshape(x.shape)


def wide(value, width):
    return jnp.concatenate([value] * (width // 128), axis=1)


def eliminate(groups, lane, step):
    width = groups[0].shape[1]
    sublane = lax.broadcasted_iota(jnp.int32, (8, 1), 0)
    for j in range(0, 8 * len(groups), step):
        home, first = j // 8, j % 8
        own = groups[home]
        low = [[None] * step for _ in range(step)]
        scales = []
        for b in range(step):
            at = lane + j + b
            column = jnp.broadcast_to(own[:, at : at + 1], (8, 128))
            for a in range(b, step):
                v = jnp.broadcast_to(column[first + a : first + a + 1, :], (8, 128))
                for c in range(b):
                    v = v - low[a][c] * low[b][c]
                if a == b:
                    scales.append(lax.rsqrt(v))
                else:
                    low[a][b] = v * scales[b]
        rows = []
        for a in range(step):
            v = jnp.broadcast_to(own[first + a : first + a + 1, :], (8, width))
            for c in range(a):
                v = v - wide(low[a][c], width) * rows[c]
            rows.append(v * wide(scales[a], width))
        for g in range(home, len(groups)):
            value = groups[g]
            if g > home or first + step < 8:
                columns = []
                new = value
                for b in range(step):
                    at = lane + j + b
                    v = jnp.broadcast_to(value[:, at : at + 1], (8, 128))
                    for c in range(b):
                        v = v - columns[c] * low[b][c]
                    columns.append(v * scales[b])
                    new = new - wide(columns[b], width) * rows[b]
                value = jnp.where(sublane >= first + step, new, value) if g == home else new
            if g == home:
                for a in range(step):
                    value = jnp.where(sublane == first + a, rows[a], value)
            groups[g] = value
    return groups


def orthonormalize_kernel(block, step, gram_ref, images_ref, out_ref, work, upper):
    n, m = gram_ref.shape[0], images_ref.shape[0]
    rows = lax.broadcasted_iota(jnp.int32, (n, n), 0)
    cols = lax.broadcasted_iota(jnp.int32, (n, n), 1)
    work[:, :n] = gram_ref[...] * (1 / NMU) + jnp.where(rows == cols, 1.0, 0.0)
    padding = jnp.zeros((128 - m, n), jnp.float32)
    work[:, n:] = jnp.concatenate([images_ref[...], padding], axis=0).T
    for k in range(0, n, block):
        t = k // 128 * 128
        groups = [work[k + g : k + g + 8, t:] for g in range(0, block, 8)]
        done = jnp.concatenate(eliminate(groups, k - t, step), axis=0)
        upper[k : k + block, :] = done[:, n - t :]
        r = (k + block) // 128 * 128
        if k + block < n:
            work[r:, r:] -= lax.dot_general(
                done[:, r - t : n - t],
                done[:, r - t :],
                (((0,), (0,)), ((), ())),
                precision=lax.Precision.HIGHEST,
                preferred_element_type=jnp.float32,
            )
    out_ref[...] = upper[...].T[:m, :]


def orthonormalize(gram_sum, images):
    n, m = gram_sum.shape[0], images.shape[0]
    return pl.pallas_call(
        functools.partial(orthonormalize_kernel, 64, 8),
        out_shape=jax.ShapeDtypeStruct((m, n), jnp.float32),
        in_specs=[pl.BlockSpec(memory_space=pltpu.VMEM)] * 2,
        out_specs=pl.BlockSpec(memory_space=pltpu.VMEM),
        scratch_shapes=[
            pltpu.VMEM((n, n + 128), jnp.float32),
            pltpu.VMEM((n, 128), jnp.float32),
        ],
    )(gram_sum, images)


def per_device(orbitals, coulomb, applied):
    width = orbitals.shape[1]
    paired = spread(jnp.concatenate([orbitals, applied], axis=1), PLANE)
    paired = paired.reshape(-1, paired.shape[-1])
    points, late = gather_z(orbitals)
    tile = swap_sides(coulomb, orbitals.shape[0], late)
    density = jnp.einsum(
        "ik,jk->ij", points, paired[:, :width], preferred_element_type=jnp.float32
    )
    kernel = (tile.astype(jnp.float32) * density).astype(jnp.bfloat16)
    images = reduce_rows(
        jnp.dot(kernel, paired[:, width:], preferred_element_type=jnp.float32)
    )
    local_gram = jnp.einsum("ia,ib->ab", images, images, precision=lax.Precision.HIGHEST)
    return orthonormalize(sum_everywhere(local_gram), images)


def solution(mesh):
    fine = Mesh(mesh.devices.reshape(SIZES), AXES)
    return jax.shard_map(
        per_device,
        mesh=fine,
        in_specs=(P(AXES, None), P(ROW, COL), P(AXES, None)),
        out_specs=P(AXES, None),
        check_vma=False,
    )
```

```python
import functools

import jax
import jax.numpy as jnp
from jax import lax
from jax.experimental import pallas as pl
from jax.experimental.pallas import tpu as pltpu
from jax.sharding import Mesh
from jax.sharding import PartitionSpec as P

NMU = 16384
ROW = ("x_hi", "y", "core")
COL = ("z", "x_lo")
PLANE = ("x_lo",) + ROW
CHIPS = ("x_lo", "y", "x_hi")
AXES = ROW + COL
SIZES = (2, 4, 2, 16, 2)


def exchange(chunks, axes):
    return lax.all_to_all(chunks, axes, 0, 0, tiled=True)


def spread(x, axes):
    copies = jnp.broadcast_to(x[None], (lax.axis_size(axes),) + x.shape)
    return exchange(copies, axes)


def after(value, *others):
    return lax.optimization_barrier((value,) + others)[0]


def gather_points(orbitals, applied, coulomb):
    n = lax.axis_size("z")
    z = lax.axis_index("z")
    rows, width = orbitals.shape
    up = [(i, (i + 1) % n) for i in range(n)]
    down = [(i, (i - 1) % n) for i in range(n)]
    mine = jnp.concatenate([orbitals, applied], axis=1)
    turned = lax.ppermute(mine, ("x_hi", "core"), [(0, 0), (1, 2), (2, 1), (3, 3)])
    own = spread(turned, CHIPS)
    kept, moved = swap_sides(coulomb, rows)
    block = jnp.zeros((n * rows, width), orbitals.dtype)
    block = lax.dynamic_update_slice(block, orbitals, (z * rows, 0))
    ahead, behind = orbitals, orbitals
    for step in range(1, n // 2 + 1):
        ahead = lax.ppermute(ahead, "z", up)
        if step < n // 2:
            behind = lax.ppermute(behind, "z", down)
            block = lax.dynamic_update_slice(block, behind, (((z + step) & (n - 1)) * rows, 0))
        block = lax.dynamic_update_slice(block, ahead, (((z - step) & (n - 1)) * rows, 0))
        if step == n // 2 - 2:
            own = after(own, behind).reshape(-1, width + applied.shape[1])
            other = lax.ppermute(own, "core", [(0, 1), (1, 0)])
        if step == n // 2 - 1:
            other = after(other, behind)
            moved = after(moved, behind)
    return block, own, other, order_tile(kept, moved)


def swap_sides(coulomb, count):
    halves = coulomb.reshape(-1, 2, count, coulomb.shape[1])
    first, second = halves[:, 0], halves[:, 1]
    low = lax.axis_index("x_lo") == 0
    kept = jnp.where(low, first, second)
    moved = lax.ppermute(jnp.where(low, second, first), "x_lo", [(0, 1), (1, 0)])
    return kept, moved


def order_tile(kept, moved):
    low = lax.axis_index("x_lo") == 0
    same = lax.axis_index("core") == 0
    half = kept.shape[-1] // 2
    left, right = jnp.where(low, kept, moved), jnp.where(low, moved, kept)
    tiles = []
    for flag in (same, jnp.logical_not(same)):
        parts = [jnp.where(flag, x[..., :half], x[..., half:]) for x in (left, right)]
        tiles.append(jnp.concatenate(parts, axis=-1).reshape(-1, 2 * half))
    return tiles


def reduce_rows(partial):
    chunks = partial.astype(jnp.bfloat16).reshape(lax.axis_size("z"), -1, partial.shape[1])
    return jnp.sum(exchange(chunks, "z").astype(jnp.float32), axis=0)


def sum_everywhere(x):
    n = lax.axis_size(PLANE)
    share = jnp.sum(exchange(x.reshape(n, -1, x.shape[1]), PLANE), axis=0)
    share = jnp.sum(spread(share, "z"), axis=0)
    return spread(share, PLANE).reshape(x.shape)


def wide(value, width):
    return jnp.concatenate([value] * (width // 128), axis=1)


def eliminate(groups, lane, step):
    width = groups[0].shape[1]
    sublane = lax.broadcasted_iota(jnp.int32, (8, 1), 0)
    for j in range(0, 8 * len(groups), step):
        home, first = j // 8, j % 8
        own = groups[home]
        low = [[None] * step for _ in range(step)]
        scales = []
        for b in range(step):
            at = lane + j + b
            column = jnp.broadcast_to(own[:, at : at + 1], (8, 128))
            for a in range(b, step):
                v = jnp.broadcast_to(column[first + a : first + a + 1, :], (8, 128))
                for c in range(b):
                    v = v - low[a][c] * low[b][c]
                if a == b:
                    scales.append(lax.rsqrt(v))
                else:
                    low[a][b] = v * scales[b]
        rows = []
        for a in range(step):
            v = jnp.broadcast_to(own[first + a : first + a + 1, :], (8, width))
            for c in range(a):
                v = v - wide(low[a][c], width) * rows[c]
            rows.append(v * wide(scales[a], width))
        for g in range(home, len(groups)):
            value = groups[g]
            if g > home or first + step < 8:
                columns = []
                new = value
                for b in range(step):
                    at = lane + j + b
                    v = jnp.broadcast_to(value[:, at : at + 1], (8, 128))
                    for c in range(b):
                        v = v - columns[c] * low[b][c]
                    columns.append(v * scales[b])
                    new = new - wide(columns[b], width) * rows[b]
                value = jnp.where(sublane >= first + step, new, value) if g == home else new
            if g == home:
                for a in range(step):
                    value = jnp.where(sublane == first + a, rows[a], value)
            groups[g] = value
    return groups


def orthonormalize_kernel(block, step, gram_ref, images_ref, out_ref, work, upper):
    n, m = gram_ref.shape[0], images_ref.shape[0]
    rows = lax.broadcasted_iota(jnp.int32, (n, n), 0)
    cols = lax.broadcasted_iota(jnp.int32, (n, n), 1)
    work[:, :n] = gram_ref[...] * (1 / NMU) + jnp.where(rows == cols, 1.0, 0.0)
    padding = jnp.zeros((128 - m, n), jnp.float32)
    work[:, n:] = jnp.concatenate([images_ref[...], padding], axis=0).T
    for k in range(0, n, block):
        t = k // 128 * 128
        groups = [work[k + g : k + g + 8, t:] for g in range(0, block, 8)]
        done = jnp.concatenate(eliminate(groups, k - t, step), axis=0)
        upper[k : k + block, :] = done[:, n - t :]
        r = (k + block) // 128 * 128
        if k + block < n:
            work[r:, r:] -= lax.dot_general(
                done[:, r - t : n - t],
                done[:, r - t :],
                (((0,), (0,)), ((), ())),
                precision=lax.Precision.HIGHEST,
                preferred_element_type=jnp.float32,
            )
    out_ref[...] = upper[...].T[:m, :]


def orthonormalize(gram_sum, images):
    n, m = gram_sum.shape[0], images.shape[0]
    return pl.pallas_call(
        functools.partial(orthonormalize_kernel, 64, 8),
        out_shape=jax.ShapeDtypeStruct((m, n), jnp.float32),
        in_specs=[pl.BlockSpec(memory_space=pltpu.VMEM)] * 2,
        out_specs=pl.BlockSpec(memory_space=pltpu.VMEM),
        scratch_shapes=[
            pltpu.VMEM((n, n + 128), jnp.float32),
            pltpu.VMEM((n, 128), jnp.float32),
        ],
    )(gram_sum, images)


def per_device(orbitals, coulomb, applied):
    width = orbitals.shape[1]
    points, own, other, tiles = gather_points(orbitals, applied, coulomb)
    partial = 0.0
    for theirs, tile in zip((own, other), tiles):
        density = jnp.einsum(
            "ik,jk->ij", points, theirs[:, :width], preferred_element_type=jnp.float32
        )
        kernel = (tile.astype(jnp.float32) * density).astype(jnp.bfloat16)
        partial += jnp.dot(kernel, theirs[:, width:], preferred_element_type=jnp.float32)
    images = reduce_rows(partial)
    local_gram = jnp.einsum("ia,ib->ab", images, images, precision=lax.Precision.HIGHEST)
    return orthonormalize(sum_everywhere(local_gram), images)


def solution(mesh):
    fine = Mesh(mesh.devices.reshape(SIZES), AXES)
    return jax.shard_map(
        per_device,
        mesh=fine,
        in_specs=(P(AXES, None), P(ROW, COL), P(AXES, None)),
        out_specs=P(AXES, None),
        check_vma=False,
    )
```

```python
import functools

import jax
import jax.numpy as jnp
from jax import lax
from jax.experimental import pallas as pl
from jax.experimental.pallas import tpu as pltpu
from jax.sharding import Mesh
from jax.sharding import PartitionSpec as P

NMU = 16384
ROW = ("x_hi", "y", "core")
COL = ("z", "x_lo")
PLANE = ("x_lo",) + ROW
CHIPS = ("x_lo", "y", "x_hi")
AXES = ROW + COL
SIZES = (2, 4, 2, 16, 2)


def exchange(chunks, axes):
    return lax.all_to_all(chunks, axes, 0, 0, tiled=True)


def spread(x, axes):
    copies = jnp.broadcast_to(x[None], (lax.axis_size(axes),) + x.shape)
    return exchange(copies, axes)


def after(value, *others):
    return lax.optimization_barrier((value,) + others)[0]


def gather_points(orbitals, applied, coulomb):
    n = lax.axis_size("z")
    rows, width = orbitals.shape

    def shifted(value, hops):
        return lax.ppermute(value, "z", [(i, (i + hops) % n) for i in range(n)])

    mine = jnp.concatenate([orbitals, applied], axis=1)
    turned = lax.ppermute(mine, ("x_hi", "core"), [(0, 0), (1, 2), (2, 1), (3, 3)])
    kept, moved = swap_sides(coulomb, rows)
    blocks = {0: orbitals}
    far, back = orbitals, orbitals
    for turn in range(1, n // 4 + 1):
        reach = 2 * turn
        near, far = shifted(far, 1), shifted(far, 2)
        if turn < n // 4:
            close, back = shifted(back, -1), shifted(back, -2)
            if turn == n // 4 - 1:
                far, moved = lax.optimization_barrier((far, moved))
            near, far, close, back = lax.optimization_barrier((near, far, close, back))
            blocks[reach - 1], blocks[reach] = close, back
        else:
            blocks[reach - 1] = shifted(back, -1)
        blocks[1 - reach], blocks[-reach] = near, far
        if turn == 1:
            own = spread(after(turned, far), CHIPS)
        if turn == n // 4 - 1:
            own = after(own, far).reshape(-1, width + applied.shape[1])
            other = lax.ppermute(own, "core", [(0, 1), (1, 0)])
    return blocks, own, other, kept, moved


def swap_sides(coulomb, count):
    halves = coulomb.reshape(-1, 2, count, coulomb.shape[1])
    first, second = halves[:, 0], halves[:, 1]
    low = lax.axis_index("x_lo") == 0
    kept = jnp.where(low, first, second)
    moved = lax.ppermute(jnp.where(low, second, first), "x_lo", [(0, 1), (1, 0)])
    return kept.reshape(-1, coulomb.shape[1]), moved.reshape(-1, coulomb.shape[1])


def images_kernel(offsets, step, place_ref, own_ref, other_ref, kept_ref, moved_ref, *refs):
    blocks, (out_ref, points, arrived) = refs[:-3], refs[-3:]
    count, width = blocks[0].shape
    place = place_ref[0]
    z, low, same = place // 4, place % 4 // 2 == 0, place % 2 == 0
    copies = []
    for i, (offset, block) in enumerate(zip(offsets, blocks)):
        at = pl.multiple_of(((z + offset) & (len(offsets) - 1)) * count, count)
        copies.append(pltpu.make_async_copy(block, points.at[pl.ds(at, count), :], arrived.at[i]))
        copies[-1].start()
    for copy in copies:
        copy.wait()
    half = kept_ref.shape[1] // 2
    for top in range(0, points.shape[0], step):
        rows = pl.ds(top, step)
        total = None
        for theirs, flag in ((own_ref, same), (other_ref, jnp.logical_not(same))):
            density = lax.dot_general(
                points[rows, :],
                theirs[:, :width],
                (((1,), (1,)), ((), ())),
                preferred_element_type=jnp.float32,
            )
            mine = jnp.where(flag, kept_ref[rows, :half], kept_ref[rows, half:])
            sent = jnp.where(flag, moved_ref[rows, :half], moved_ref[rows, half:])
            tile = jnp.concatenate(
                [jnp.where(low, mine, sent), jnp.where(low, sent, mine)], axis=1
            )
            kernel = (tile.astype(jnp.float32) * density).astype(jnp.bfloat16)
            part = jnp.dot(kernel, theirs[:, width:], preferred_element_type=jnp.float32)
            total = part if total is None else total + part
        out_ref[rows, :] = total.astype(jnp.bfloat16)


def partial_images(place, blocks, own, other, kept, moved):
    offsets = sorted(blocks)
    count, width = blocks[0].shape
    rows = len(offsets) * count
    vmem = pl.BlockSpec(memory_space=pltpu.VMEM)
    return pl.pallas_call(
        functools.partial(images_kernel, offsets, 256),
        out_shape=jax.ShapeDtypeStruct((rows, own.shape[1] - width), jnp.bfloat16),
        in_specs=[pl.BlockSpec(memory_space=pltpu.SMEM)]
        + [vmem] * 4
        + [pl.BlockSpec(memory_space=pl.ANY)] * len(offsets),
        out_specs=vmem,
        scratch_shapes=[
            pltpu.VMEM((rows, width), jnp.bfloat16),
            pltpu.SemaphoreType.DMA((len(offsets),)),
        ],
        compiler_params=pltpu.CompilerParams(vmem_limit_bytes=24 << 20),
    )(place, own, other, kept, moved, *[blocks[offset] for offset in offsets])


def reduce_rows(partial):
    chunks = partial.reshape(lax.axis_size("z"), -1, partial.shape[1])
    return jnp.sum(exchange(chunks, "z").astype(jnp.float32), axis=0)


def sum_everywhere(x):
    n = lax.axis_size(PLANE)
    share = jnp.sum(exchange(x.reshape(n, -1, x.shape[1]), PLANE), axis=0)
    share = jnp.sum(spread(share, "z"), axis=0)
    return spread(share, PLANE).reshape(x.shape)


def wide(value, width):
    return jnp.concatenate([value] * (width // 128), axis=1)


def eliminate(groups, lane, step):
    width = groups[0].shape[1]
    sublane = lax.broadcasted_iota(jnp.int32, (8, 1), 0)
    for j in range(0, 8 * len(groups), step):
        home, first = j // 8, j % 8
        own = groups[home]
        low = [[None] * step for _ in range(step)]
        scales = []
        for b in range(step):
            at = lane + j + b
            column = jnp.broadcast_to(own[:, at : at + 1], (8, 128))
            for a in range(b, step):
                v = jnp.broadcast_to(column[first + a : first + a + 1, :], (8, 128))
                for c in range(b):
                    v = v - low[a][c] * low[b][c]
                if a == b:
                    scales.append(lax.rsqrt(v))
                else:
                    low[a][b] = v * scales[b]
        rows = []
        for a in range(step):
            v = jnp.broadcast_to(own[first + a : first + a + 1, :], (8, width))
            for c in range(a):
                v = v - wide(low[a][c], width) * rows[c]
            rows.append(v * wide(scales[a], width))
        for g in range(home, len(groups)):
            value = groups[g]
            if g > home or first + step < 8:
                columns = []
                new = value
                for b in range(step):
                    at = lane + j + b
                    v = jnp.broadcast_to(value[:, at : at + 1], (8, 128))
                    for c in range(b):
                        v = v - columns[c] * low[b][c]
                    columns.append(v * scales[b])
                    new = new - wide(columns[b], width) * rows[b]
                value = jnp.where(sublane >= first + step, new, value) if g == home else new
            if g == home:
                for a in range(step):
                    value = jnp.where(sublane == first + a, rows[a], value)
            groups[g] = value
    return groups


def orthonormalize_kernel(block, step, gram_ref, images_ref, out_ref, work, upper):
    n, m = gram_ref.shape[0], images_ref.shape[0]
    rows = lax.broadcasted_iota(jnp.int32, (n, n), 0)
    cols = lax.broadcasted_iota(jnp.int32, (n, n), 1)
    work[:, :n] = gram_ref[...] * (1 / NMU) + jnp.where(rows == cols, 1.0, 0.0)
    padding = jnp.zeros((128 - m, n), jnp.float32)
    work[:, n:] = jnp.concatenate([images_ref[...], padding], axis=0).T
    for k in range(0, n, block):
        t = k // 128 * 128
        groups = [work[k + g : k + g + 8, t:] for g in range(0, block, 8)]
        done = jnp.concatenate(eliminate(groups, k - t, step), axis=0)
        upper[k : k + block, :] = done[:, n - t :]
        r = (k + block) // 128 * 128
        if k + block < n:
            work[r:, r:] -= lax.dot_general(
                done[:, r - t : n - t],
                done[:, r - t :],
                (((0,), (0,)), ((), ())),
                precision=lax.Precision.HIGHEST,
                preferred_element_type=jnp.float32,
            )
    out_ref[...] = upper[...].T[:m, :]


def orthonormalize(gram_sum, images):
    n, m = gram_sum.shape[0], images.shape[0]
    return pl.pallas_call(
        functools.partial(orthonormalize_kernel, 64, 8),
        out_shape=jax.ShapeDtypeStruct((m, n), jnp.float32),
        in_specs=[pl.BlockSpec(memory_space=pltpu.VMEM)] * 2,
        out_specs=pl.BlockSpec(memory_space=pltpu.VMEM),
        scratch_shapes=[
            pltpu.VMEM((n, n + 128), jnp.float32),
            pltpu.VMEM((n, 128), jnp.float32),
        ],
    )(gram_sum, images)


def per_device(orbitals, coulomb, applied):
    side, core = lax.axis_index("x_lo"), lax.axis_index("core")
    place = (lax.axis_index("z") * 4 + side * 2 + core).reshape(1)
    gathered = gather_points(orbitals, applied, coulomb)
    partial = partial_images(place, *gathered)
    images = reduce_rows(partial)
    local_gram = jnp.einsum("ia,ib->ab", images, images, precision=lax.Precision.HIGHEST)
    return orthonormalize(sum_everywhere(local_gram), images)


def solution(mesh):
    fine = Mesh(mesh.devices.reshape(SIZES), AXES)
    return jax.shard_map(
        per_device,
        mesh=fine,
        in_specs=(P(AXES, None), P(ROW, COL), P(AXES, None)),
        out_specs=P(AXES, None),
        check_vma=False,
    )
```

```python
import functools

import jax
import jax.numpy as jnp
from jax import lax
from jax.experimental import pallas as pl
from jax.experimental.pallas import tpu as pltpu
from jax.sharding import Mesh
from jax.sharding import PartitionSpec as P


NMU = 16384
ROW = ("x_hi", "y", "core")
COL = ("z", "x_lo")
PLANE = ("x_lo",) + ROW
AXES = ROW + COL
SIZES = (2, 4, 2, 16, 2)


def exchange(chunks, axes):
    return lax.all_to_all(chunks, axes, 0, 0, tiled=True)


def spread(x, axes):
    copies = jnp.broadcast_to(x[None], (lax.axis_size(axes),) + x.shape)
    return exchange(copies, axes)


def after(value, *others):
    return lax.optimization_barrier((value,) + others)[0]


def gather_z(mine):
    n = lax.axis_size("z")
    z = lax.axis_index("z")
    rows = mine.shape[0]
    block = jnp.zeros((n * rows, mine.shape[1]), mine.dtype)
    block = lax.dynamic_update_slice(block, mine, (z * rows, 0))
    up = [(i, (i + 1) % n) for i in range(n)]
    down = [(i, (i - 1) % n) for i in range(n)]
    ahead, behind = mine, mine
    for step in range(1, n // 2 + 1):
        if step == n // 2:
            ahead, behind = ahead[: rows // 2], behind[rows // 2 :]
        ahead = lax.ppermute(ahead, "z", up)
        behind = lax.ppermute(behind, "z", down)
        at = ((z + step) & (n - 1)) * rows
        if step == n // 2:
            block = lax.dynamic_update_slice(block, behind, (at + rows // 2, 0))
        else:
            block = lax.dynamic_update_slice(block, behind, (at, 0))
            late = ahead
        block = lax.dynamic_update_slice(block, ahead, (((z - step) & (n - 1)) * rows, 0))
    return block, late


def swap_sides(coulomb, count, late):
    side = lax.axis_index("x_lo")
    halves = coulomb.reshape(-1, 2, count, coulomb.shape[1])
    first, second = halves[:, 0], halves[:, 1]
    low = side == 0
    kept = jnp.where(low, first, second)
    moved = lax.ppermute(jnp.where(low, second, first), "x_lo", [(0, 1), (1, 0)])
    moved = after(moved, late)
    left, right = jnp.where(low, kept, moved), jnp.where(low, moved, kept)
    return jnp.concatenate([left, right], axis=-1).reshape(-1, 2 * coulomb.shape[1])


def reduce_rows(partial):
    chunks = partial.astype(jnp.bfloat16).reshape(lax.axis_size("z"), -1, partial.shape[1])
    return jnp.sum(exchange(chunks, "z").astype(jnp.float32), axis=0)


def sum_everywhere(x):
    n = lax.axis_size(PLANE)
    share = jnp.sum(exchange(x.reshape(n, -1, x.shape[1]), PLANE), axis=0)
    share = jnp.sum(spread(share, "z"), axis=0)
    return spread(share, PLANE).reshape(x.shape)


def wide(value, width):
    return jnp.concatenate([value] * (width // 128), axis=1)


def eliminate(groups, lane, step):
    width = groups[0].shape[1]
    sublane = lax.broadcasted_iota(jnp.int32, (8, 1), 0)
    for j in range(0, 8 * len(groups), step):
        home, first = j // 8, j % 8
        own = groups[home]
        low = [[None] * step for _ in range(step)]
        scales = []
        for b in range(step):
            at = lane + j + b
            column = jnp.broadcast_to(own[:, at : at + 1], (8, 128))
            for a in range(b, step):
                v = jnp.broadcast_to(column[first + a : first + a + 1, :], (8, 128))
                for c in range(b):
                    v = v - low[a][c] * low[b][c]
                if a == b:
                    scales.append(lax.rsqrt(v))
                else:
                    low[a][b] = v * scales[b]
        rows = []
        for a in range(step):
            v = jnp.broadcast_to(own[first + a : first + a + 1, :], (8, width))
            for c in range(a):
                v = v - wide(low[a][c], width) * rows[c]
            rows.append(v * wide(scales[a], width))
        for g in range(home, len(groups)):
            value = groups[g]
            if g > home or first + step < 8:
                columns = []
                new = value
                for b in range(step):
                    at = lane + j + b
                    v = jnp.broadcast_to(value[:, at : at + 1], (8, 128))
                    for c in range(b):
                        v = v - columns[c] * low[b][c]
                    columns.append(v * scales[b])
                    new = new - wide(columns[b], width) * rows[b]
                value = jnp.where(sublane >= first + step, new, value) if g == home else new
            if g == home:
                for a in range(step):
                    value = jnp.where(sublane == first + a, rows[a], value)
            groups[g] = value
    return groups


def orthonormalize_kernel(block, step, gram_ref, images_ref, out_ref, work, upper):
    n, m = gram_ref.shape[0], images_ref.shape[0]
    rows = lax.broadcasted_iota(jnp.int32, (n, n), 0)
    cols = lax.broadcasted_iota(jnp.int32, (n, n), 1)
    work[:, :n] = gram_ref[...] * (1 / NMU) + jnp.where(rows == cols, 1.0, 0.0)
    padding = jnp.zeros((128 - m, n), jnp.float32)
    work[:, n:] = jnp.concatenate([images_ref[...], padding], axis=0).T
    for k in range(0, n, block):
        t = k // 128 * 128
        groups = [work[k + g : k + g + 8, t:] for g in range(0, block, 8)]
        done = jnp.concatenate(eliminate(groups, k - t, step), axis=0)
        upper[k : k + block, :] = done[:, n - t :]
        r = (k + block) // 128 * 128
        if k + block < n:
            work[r:, r:] -= lax.dot_general(
                done[:, r - t : n - t],
                done[:, r - t :],
                (((0,), (0,)), ((), ())),
                precision=lax.Precision.HIGHEST,
                preferred_element_type=jnp.float32,
            )
    out_ref[...] = upper[...].T[:m, :]


def orthonormalize(gram_sum, images):
    n, m = gram_sum.shape[0], images.shape[0]
    return pl.pallas_call(
        functools.partial(orthonormalize_kernel, 64, 8),
        out_shape=jax.ShapeDtypeStruct((m, n), jnp.float32),
        in_specs=[pl.BlockSpec(memory_space=pltpu.VMEM)] * 2,
        out_specs=pl.BlockSpec(memory_space=pltpu.VMEM),
        scratch_shapes=[
            pltpu.VMEM((n, n + 128), jnp.float32),
            pltpu.VMEM((n, 128), jnp.float32),
        ],
    )(gram_sum, images)


def per_device(orbitals, coulomb, applied):
    width = orbitals.shape[1]
    paired = spread(jnp.concatenate([orbitals, applied], axis=1), PLANE)
    paired = paired.reshape(-1, paired.shape[-1])
    points, late = gather_z(orbitals)
    tile = swap_sides(coulomb, orbitals.shape[0], late)
    density = jnp.einsum(
        "ik,jk->ij", points, paired[:, :width], preferred_element_type=jnp.float32
    )
    kernel = (tile.astype(jnp.float32) * density).astype(jnp.bfloat16)
    images = reduce_rows(
        jnp.dot(kernel, paired[:, width:], preferred_element_type=jnp.float32)
    )
    local_gram = jnp.einsum("ia,ib->ab", images, images, precision=lax.Precision.HIGHEST)
    return orthonormalize(sum_everywhere(local_gram), images)


def solution(mesh):
    fine = Mesh(mesh.devices.reshape(SIZES), AXES)

    return jax.shard_map(
        per_device,
        mesh=fine,
        in_specs=(P(AXES, None), P(ROW, COL), P(AXES, None)),
        out_specs=P(AXES, None),
        check_vma=False,
    )
```
